32 devices in a mesh: section: 2 (over core), seq: 16 (over z, y, x).
Axes of the slice: x: 2, y: 2, z: 4, core: 2. Of those that a mesh axis runs over, the one named last changes fastest.
Arguments:
- tokens: bfloat16 [1, 2048, 1024], P(None, 'seq'), may hold values from -24 to 24
- neighbor_ids: int32 [16, 9], P('seq'), may hold values from 0 to 15, as said below
- neighbor_count: int32 [16], P('seq'), may hold values from 1 to 9, as said below
- w_query: bfloat16 [2, 1024, 1024], P('section')
- w_key: bfloat16 [2, 1024, 1024], P('section')
- w_value: bfloat16 [2, 1024, 1024], P('section'), may hold values from -0.1875 to 0.1875
- w_out: bfloat16 [2, 1024, 1024], P('section'), may hold values from -0.1875 to 0.1875
- norm_gain: float32 [2, 1024], P('section'), may hold values from 0.5 to 3
- w_up: bfloat16 [2, 4096, 1024], P('section', 'seq'), may hold values from -0.1875 to 0.1875
- w_down: bfloat16 [2, 4096, 1024], P('section', 'seq'), may hold values from -0.09375 to 0.09375
- mlp_gain: float32 [2, 1024], P('section'), may hold values from 0.5 to 2
Outputs:
- layer_outputs: bfloat16 [2, 1, 2048, 1024], P('section', None, 'seq')
The draws below stay inside these ranges and needn't reach their ends.
Inputs may be any that keep to these rules, and one draw needn't show every extreme that they name: `neighbor_ids`: blocks lie row by row on a map 4 blocks wide. Row b lists in its first neighbor_count[b] entries distinct blocks among b and the up to eight blocks beside it on the map (diagonals included), b first; its other entries equal b. `neighbor_count`: some block has 9.
All inputs are finite; a program needn't handle non-finite values.
Results may differ from the reference program's by a relative error of at most 0.017.
Values may be sent and summed in bfloat16 or wider, within the bound.
A program may use at most 128 MiB of HBM per device.

```python
import math
import jax
import jax.numpy as jnp
from jax import lax

D = 1024
HEADS = 16
FF = 4096
HD = 64
BLK = 128
ROW = 4
MAXN = 9
GRAPHS = 1
LAYERS = 2
TOKENS = 2048
NBLK = 16


def neighbor_table(key):
    blocks = jnp.arange(NBLK, dtype=jnp.int32)
    grid_row = blocks // ROW
    grid_col = blocks % ROW
    step_row = jnp.array([0, -1, -1, -1, 0, 0, 1, 1, 1], dtype=jnp.int32)
    step_col = jnp.array([0, -1, 0, 1, -1, 1, -1, 0, 1], dtype=jnp.int32)
    near_row = grid_row[:, None] + step_row[None, :]
    near_col = grid_col[:, None] + step_col[None, :]
    inside = (near_row >= 0) & (near_row < NBLK // ROW) & (near_col >= 0) & (near_col < ROW)
    keep_link = jax.random.randint(key, (NBLK, 9), 0, 10) < 7
    keep_link = keep_link.at[:, 0].set(True)
    dense_block = (blocks == ROW + 1)[:, None]
    linked = inside & (keep_link | dense_block)
    near_ids = near_row * ROW + near_col
    ordering = jnp.argsort(jnp.where(linked, 0, 1) * 16 + jnp.arange(9, dtype=jnp.int32)[None, :], axis=1)
    sorted_ids = jnp.take_along_axis(near_ids, ordering, axis=1)
    sorted_live = jnp.take_along_axis(linked, ordering, axis=1)
    final_ids = jnp.where(sorted_live, sorted_ids, blocks[:, None])
    counts = jnp.sum(linked.astype(jnp.int32), axis=1)
    return (final_ids.astype(jnp.int32), counts.astype(jnp.int32))


def draw_neighbor_ids(key, part):
    return neighbor_table(jax.random.fold_in(key, 11))[0]


def draw_neighbor_count(key, part):
    return neighbor_table(jax.random.fold_in(key, 11))[1]


def query_base(key):
    return jax.random.normal(jax.random.fold_in(key, 21), (LAYERS, D, D), jnp.float32) / math.sqrt(D)


def draw_w_query(key, part):
    return (1.6 * query_base(key)).astype(jnp.bfloat16)


def draw_w_key(key, part):
    other = jax.random.normal(jax.random.fold_in(key, 22), (LAYERS, D, D), jnp.float32) / math.sqrt(D)
    mixture = 1.6 * other
    return mixture.astype(jnp.bfloat16)


def draw_norm_gain(key, part):
    values = jax.random.uniform(jax.random.fold_in(key, 31), (LAYERS, D), jnp.float32, 0.5, 1.5)
    return values


def draw_tokens(key, part):
    values = jax.random.normal(jax.random.fold_in(key, 41), (GRAPHS, TOKENS, D), jnp.float32)
    return jnp.clip(values, -24.0, 24.0).astype(jnp.bfloat16)


def block_scale(key, extent, shards, smallest, top_value):
    def one(dim, shards_of):
        draws = jax.random.uniform(jax.random.fold_in(jax.random.fold_in(key, 6), dim), (shards_of,), jnp.float32, smallest / len(shards), top_value / len(shards))
        return jnp.repeat(jnp.exp(draws), extent[dim] // shards_of).reshape((-1,) + (1,) * (len(extent) - dim - 1))

    loudness = one(*shards[0])
    for cut in shards[1:]:
        loudness = loudness * one(*cut)
    return loudness


def centred(key, shape, spread, reach, split=(), held_as=jnp.bfloat16):
    result = spread * jax.random.normal(key, shape, jnp.float32)
    if split:
        result = result * block_scale(key, shape, split, -0.22, 0.18)
    return jnp.clip(result, -reach, reach).astype(held_as)


def setup_inputs(seed: int = 0) -> dict:
    key_list = jax.random.split(jax.random.key(seed), 12)
    tokens = draw_tokens(jax.random.fold_in(key_list[11], 71), 0)
    neighbor_ids = draw_neighbor_ids(jax.random.fold_in(key_list[11], 71), 0)
    neighbor_count = draw_neighbor_count(jax.random.fold_in(key_list[11], 71), 0)
    w_query = draw_w_query(jax.random.fold_in(key_list[11], 71), 0)
    w_key = draw_w_key(jax.random.fold_in(key_list[11], 71), 0)
    w_value = centred(key_list[5], (LAYERS, D, D), D ** -0.5, 0.1875, ((0, 2),))
    w_out = centred(key_list[6], (LAYERS, D, D), D ** -0.5, 0.1875, ((0, 2),))
    norm_gain = draw_norm_gain(jax.random.fold_in(key_list[11], 71), 0)
    w_up = centred(key_list[8], (LAYERS, FF, D), D ** -0.5, 0.1875, ((0, 2), (1, 16)))
    w_down = centred(key_list[9], (LAYERS, FF, D), FF ** -0.5, 0.09375, ((0, 2), (1, 16)))
    mlp_gain = jnp.clip(jnp.exp(math.log(2.0) - 1.3862944 * jax.random.uniform(key_list[10], (LAYERS, D), jnp.float32) ** block_scale(key_list[10], (LAYERS, D), ((0, 2),), -0.2, 0.2)), 0.5, 2.0)
    return dict(tokens=tokens, neighbor_ids=neighbor_ids, neighbor_count=neighbor_count, w_query=w_query, w_key=w_key, w_value=w_value, w_out=w_out, norm_gain=norm_gain, w_up=w_up, w_down=w_down, mlp_gain=mlp_gain)


def rms_normed(widened, gain):
    return (widened * lax.rsqrt(lax.optimization_barrier(jnp.mean(widened * widened, axis=-1, keepdims=True)) + 1e-05) * gain).astype(jnp.bfloat16)

def one_layer(inputs, neighbor_ids, neighbor_count, query_weight, key_weight, value_weight, out_weight, gain, up_weight, down_weight, second_gain):
    widened = inputs.astype(jnp.float32)
    normed = rms_normed(widened, gain)
    queries = jnp.dot(normed, query_weight, preferred_element_type=jnp.float32).astype(jnp.bfloat16)
    keys = jnp.dot(normed, key_weight, preferred_element_type=jnp.float32).astype(jnp.bfloat16)
    values = jnp.dot(normed, value_weight, preferred_element_type=jnp.float32).astype(jnp.bfloat16)
    key_blocks = keys.reshape(NBLK, BLK, D)
    value_blocks = values.reshape(NBLK, BLK, D)
    score_scale = 1.0 / math.sqrt(HD)

    def one_block(block):
        query_rows = lax.dynamic_slice_in_dim(queries, block * BLK, BLK, 0).reshape(BLK, HEADS, HD).astype(jnp.float32)
        listed = neighbor_ids[block]
        key_rows = jnp.take(key_blocks, listed, axis=0).reshape(MAXN * BLK, HEADS, HD).astype(jnp.float32)
        value_rows = jnp.take(value_blocks, listed, axis=0).reshape(MAXN * BLK, HEADS, HD).astype(jnp.float32)
        live = jnp.repeat(jnp.arange(MAXN, dtype=jnp.int32) < neighbor_count[block], BLK)
        scores = jnp.einsum('qhd,khd->hqk', query_rows, key_rows) * score_scale
        scores = jnp.where(live[None, None, :], scores, -jnp.inf)
        row_max = lax.optimization_barrier(jnp.max(scores, axis=-1, keepdims=True))
        exponent = jnp.exp(scores - row_max)
        probs = (exponent / lax.optimization_barrier(jnp.sum(exponent, axis=-1, keepdims=True))).astype(jnp.bfloat16)
        mixed = jnp.einsum('hqk,khd->qhd', probs.astype(jnp.float32), value_rows).astype(jnp.bfloat16)
        return mixed.reshape(BLK, D)
    mixed = lax.map(one_block, jnp.arange(NBLK, dtype=jnp.int32)).reshape(NBLK * BLK, D)
    attended = (widened + jnp.dot(mixed, out_weight, preferred_element_type=jnp.float32)).astype(jnp.bfloat16)
    attended_wide = attended.astype(jnp.float32)
    second = rms_normed(attended_wide, second_gain)
    upper_rows = lax.dot_general(second, up_weight, (((1,), (1,)), ((), ())), preferred_element_type=jnp.float32)
    hidden = jax.nn.gelu(upper_rows, approximate=True).astype(jnp.bfloat16)
    return (attended_wide + jnp.dot(hidden, down_weight, preferred_element_type=jnp.float32)).astype(jnp.bfloat16)

def reference(tokens, neighbor_ids, neighbor_count, w_query, w_key, w_value, w_out, norm_gain, w_up, w_down, mlp_gain):
    per_layer = []
    for layer_index in range(LAYERS):
        per_layer.append([])
    for graph_index in range(GRAPHS):
        hidden_state = tokens[graph_index]
        for layer_index in range(LAYERS):
            hidden_state = one_layer(hidden_state, neighbor_ids, neighbor_count, w_query[layer_index], w_key[layer_index], w_value[layer_index], w_out[layer_index], norm_gain[layer_index], w_up[layer_index], w_down[layer_index], mlp_gain[layer_index])
            per_layer[layer_index].append(hidden_state)
    return jnp.stack([jnp.stack(items, axis=0) for items in per_layer], axis=0)
```

```python
import functools
import math

import jax
import jax.numpy as jnp
from jax import lax
from jax.experimental import pallas as pl
from jax.experimental.pallas import tpu as pltpu
from jax.sharding import PartitionSpec as P

HEADS = 16
BLK = 128
ROW = 4
GROUP = 4
TILE = 256
MESH = pl.DeviceIdType.MESH
NT = (((1,), (1,)), ((), ()))


def normalise(widened, gain):
    mean = jnp.mean(widened * widened, axis=-1, keepdims=True)
    return (widened * lax.rsqrt(mean + 1e-05) * gain).astype(jnp.bfloat16)


def kernel(
    n, ids, count, tokens, w_query, w_key, w_value, w_out, gain, w_up, w_down, second_gain,
    out,
    around, normed, queries, keys, values, mixed, attended, second, hidden, total, leaving,
    landing, finished, wq, wk, wv, wo, up, down,
    local_sem, x_send, x_recv, o_send, w_send, w_recv, s_send, s_recv, p_send, p_recv, go,
):
    section, seq = lax.axis_index("section"), lax.axis_index("seq")
    row, col = lax.div(seq, ROW), lax.rem(seq, ROW)
    rows = n // ROW
    width = wq.shape[0]
    units = w_up.shape[1]
    mine = lax.rem(row, GROUP)
    members = n // GROUP
    member = lax.div(row, GROUP) * ROW + col
    pairs = HEADS // 2
    tiles = width // TILE

    def local(src, dst, index):
        return pltpu.make_async_copy(src, dst, local_sem.at[index])

    own_up = pl.ds(pl.multiple_of(member * units, units), units)
    locals_ = [
        local(w_query.at[0], wq, 0),
        local(w_key.at[0], wk, 1),
        local(w_value.at[0], wv, 2),
        local(w_out.at[0], wo, 3),
        local(w_up.at[0], up.at[own_up], 4),
        local(w_down.at[0], down.at[own_up], 5),
    ]
    own_tokens = local(tokens.at[0], around.at[4], 6)

    @pl.when(section == 0)
    def _():
        own_tokens.start()

    for copy in locals_:
        copy.start()

    barrier = pltpu.get_barrier_semaphore()

    def greet(step, carry):
        other = lax.rem(section * n + seq + 1 + step, 2 * n)
        pl.semaphore_signal(barrier, inc=1, device_id=(lax.div(other, n), lax.rem(other, n)), device_id_type=MESH)
        return carry

    lax.fori_loop(0, 2 * n - 1, greet, 0)
    pl.semaphore_wait(barrier, 2 * n - 1)

    def beside(slot):
        dr, dc = slot // 3 - 1, slot % 3 - 1
        exists = (row + dr >= 0) & (row + dr < rows) & (col + dc >= 0) & (col + dc < ROW)
        return exists, jnp.clip(row + dr, 0, rows - 1) * ROW + jnp.clip(col + dc, 0, ROW - 1)

    def token_copy(slot):
        device = beside(slot)[1]
        return pltpu.make_async_remote_copy(
            tokens.at[0], around.at[8 - slot], x_send.at[slot], x_recv.at[8 - slot],
            device_id=(section, device), device_id_type=MESH)

    def result_copy(slot):
        device = beside(slot)[1]
        return pltpu.make_async_remote_copy(
            finished, around.at[8 - slot], o_send.at[slot], x_recv.at[8 - slot],
            device_id=(1, device), device_id_type=MESH)

    def arrival(slot):
        return pltpu.make_async_remote_copy(
            finished, around.at[slot], o_send.at[slot], x_recv.at[slot],
            device_id=(section, seq), device_id_type=MESH)

    def weight_copies(step, which):
        place = lax.rem(member + step, members)
        device = (lax.div(place, ROW) * GROUP + mine) * ROW + lax.rem(place, ROW)
        src, dst = (w_up, up) if which == 0 else (w_down, down)
        return pltpu.make_async_remote_copy(
            src.at[0], dst.at[own_up], w_send.at[2 * step + which], w_recv.at[2 * step + which],
            device_id=(section, device), device_id_type=MESH)

    def weight_arrival(step, which):
        place = lax.rem(member + members - step, members)
        there = pl.ds(pl.multiple_of(place * units, units), units)
        src, dst = (w_up, up) if which == 0 else (w_down, down)
        return pltpu.make_async_remote_copy(
            src.at[0], dst.at[there], w_send.at[2 * step + which], w_recv.at[2 * step + which],
            device_id=(section, seq), device_id_type=MESH)

    def each(body):
        if members > 8:
            lax.fori_loop(1, members, body, 0)
        else:
            for step in range(1, members):
                body(step, 0)

    @pl.when(section == 0)
    def _():
        for slot in (0, 2, 6, 8, 1, 7, 3, 5):
            @pl.when(beside(slot)[0])
            def _():
                token_copy(slot).start()

    @pl.when(section == 1)
    def _():
        pl.semaphore_wait(go, 1)

    def send_weights(step, carry):
        weight_copies(step, 0).start()
        weight_copies(step, 1).start()
        return carry

    each(send_weights)

    def await_slot(slot):
        exists = beside(slot)[0]

        @pl.when(exists)
        def _():
            arrival(slot).wait_recv()

        @pl.when(jnp.logical_not(exists))
        def _():
            around[slot] = jnp.zeros((BLK, width), jnp.bfloat16)

    @pl.when(section == 0)
    def _():
        own_tokens.wait()

    @pl.when(section == 1)
    def _():
        arrival(4).wait_recv()

    entries = ids[...]
    listed = lax.broadcasted_iota(jnp.int32, entries.shape, 1) < count[...]
    flags = []
    for slot in range(9):
        exists, device = beside(slot)
        wanted = jnp.where(exists, device, jnp.int32(-1))
        hit = jnp.where(listed & (entries == wanted), 1.0, 0.0)
        flags.append(jnp.broadcast_to(jnp.max(hit, axis=1, keepdims=True), (1, BLK)))
    live_row = jnp.concatenate(flags, axis=1)

    gain_row = gain[...]
    normed[pl.ds(0, BLK)] = normalise(around[4].astype(jnp.float32), gain_row)
    locals_[0].wait()

    score_scale = 1.0 / math.sqrt(width // HEADS)

    def query_tile(step, carry):
        at = pl.ds(pl.multiple_of(step * TILE, TILE), TILE)
        product = jnp.dot(normed[pl.ds(0, BLK)], wq[:, at], preferred_element_type=jnp.float32)
        queries[:, at] = (product.astype(jnp.bfloat16).astype(jnp.float32) * score_scale).astype(jnp.bfloat16)
        return carry

    lax.fori_loop(0, tiles, query_tile, 0)
    locals_[1].wait()
    locals_[2].wait()

    for part in (1, 0, 2):
        for slot in range(3 * part, 3 * part + 3):
            if slot != 4:
                await_slot(slot)
        for slot in range(3):
            normed[pl.ds(slot * BLK, BLK)] = normalise(
                around[3 * part + slot].astype(jnp.float32), gain_row)

        def key_tile(step, carry):
            at = pl.ds(pl.multiple_of(step * TILE, TILE), TILE)
            there = pl.ds(3 * part * BLK, 3 * BLK)
            keys[there, at] = jnp.dot(
                normed[...], wk[:, at], preferred_element_type=jnp.float32).astype(jnp.bfloat16)
            values[there, at] = jnp.dot(
                normed[...], wv[:, at], preferred_element_type=jnp.float32).astype(jnp.bfloat16)
            return carry

        lax.fori_loop(0, tiles, key_tile, 0)

    first_half = lax.broadcasted_iota(jnp.int32, (BLK, 128), 1) < 64

    def head_pair(pair, carry):
        at = pl.ds(pl.multiple_of(pair * 128, 128), 128)
        q = queries[:, at]
        zero = jnp.zeros_like(q)
        both = jnp.concatenate([jnp.where(first_half, q, zero), jnp.where(first_half, zero, q)], axis=0)
        scores = lax.dot_general(both, keys[:, at], NT, preferred_element_type=jnp.float32)
        scores = jnp.where(live_row > 0.0, scores, -jnp.inf)
        exponent = jnp.exp(scores - jnp.max(scores, axis=-1, keepdims=True))
        divisor = jnp.sum(exponent, axis=-1, keepdims=True)
        product = jnp.dot(
            exponent.astype(jnp.bfloat16), values[:, at], preferred_element_type=jnp.float32) / divisor
        mixed[:, at] = jnp.where(first_half, product[:BLK], product[BLK:]).astype(jnp.bfloat16)
        return carry

    lax.fori_loop(0, pairs, head_pair, 0)
    locals_[3].wait()

    def out_tile(step, carry):
        at = pl.ds(pl.multiple_of(step * TILE, TILE), TILE)
        product = jnp.dot(mixed[...], wo[:, at], preferred_element_type=jnp.float32)
        attended[:, at] = (around[4, :, at].astype(jnp.float32) + product).astype(jnp.bfloat16)
        return carry

    lax.fori_loop(0, tiles, out_tile, 0)
    second[mine] = normalise(attended[...].astype(jnp.float32), second_gain[...])

    def peer(step):
        return lax.rem(mine + step, GROUP)

    def peer_device(step):
        return (lax.div(row, GROUP) * GROUP + peer(step)) * ROW + col

    def second_copy(step):
        return pltpu.make_async_remote_copy(
            second.at[mine], second.at[mine], s_send.at[step], s_recv.at[step],
            device_id=(section, peer_device(step)), device_id_type=MESH)

    def second_arrival(step):
        return pltpu.make_async_remote_copy(
            second.at[mine], second.at[peer(step)], s_send.at[step], s_recv.at[GROUP - step],
            device_id=(section, peer_device(step)), device_id_type=MESH)

    def partial_copy(step):
        return pltpu.make_async_remote_copy(
            leaving.at[step], landing.at[step], p_send.at[step], p_recv.at[step],
            device_id=(section, peer_device(step)), device_id_type=MESH)

    for step in range(1, GROUP):
        second_copy(step).start()

    locals_[4].wait()
    locals_[5].wait()

    def await_weights(step, carry):
        weight_arrival(step, 0).wait_recv()
        weight_arrival(step, 1).wait_recv()
        return carry

    each(await_weights)

    @pl.when(section == 0)
    def _():
        pl.semaphore_signal(go, inc=1, device_id=(1, seq), device_id_type=MESH)

    for step in range(GROUP):
        if step:
            second_arrival(step).wait_recv()
        rows_in = second.at[peer(step)]

        def up_tile(tile, carry):
            at = pl.ds(pl.multiple_of(tile * TILE, TILE), TILE)
            raised = lax.dot_general(rows_in[...], up[at], NT, preferred_element_type=jnp.float32)
            hidden[:, at] = jax.nn.gelu(raised, approximate=True).astype(jnp.bfloat16)
            return carry

        lax.fori_loop(0, up.shape[0] // TILE, up_tile, 0)

        def down_tile(tile, carry):
            at = pl.ds(pl.multiple_of(tile * TILE, TILE), TILE)
            product = jnp.dot(hidden[...], down[:, at], preferred_element_type=jnp.float32)
            if step:
                leaving[step, :, at] = product.astype(jnp.bfloat16)
            else:
                total[:, at] = product
            return carry

        lax.fori_loop(0, tiles, down_tile, 0)
        if step:
            partial_copy(step).start()

    gathered = attended[...].astype(jnp.float32) + total[...]
    for step in range(1, GROUP):
        partial_copy(step).wait_recv()
        gathered = gathered + landing[step].astype(jnp.float32)
    result = gathered.astype(jnp.bfloat16)
    finished[...] = result
    out[0, 0] = result

    @pl.when(section == 0)
    def _():
        for slot in (0, 2, 6, 8, 1, 7, 3, 5, 4):
            @pl.when(beside(slot)[0])
            def _():
                result_copy(slot).start()
        for slot in range(9):
            @pl.when(beside(slot)[0])
            def _():
                result_copy(slot).wait_send()
                if slot != 4:
                    token_copy(slot).wait_send()

    for step in range(1, GROUP):
        second_copy(step).wait_send()
        partial_copy(step).wait_send()

    def drain(step, carry):
        weight_copies(step, 0).wait_send()
        weight_copies(step, 1).wait_send()
        return carry

    each(drain)


def solution(mesh):
    n = mesh.shape["seq"]

    def local(tokens, ids, count, w_query, w_key, w_value, w_out, gain, w_up, w_down, second_gain):
        width = tokens.shape[-1]
        held = w_up.shape[1] * n // GROUP
        members = n // GROUP
        bf16, f32 = jnp.bfloat16, jnp.float32
        any_ = pl.BlockSpec(memory_space=pl.ANY)
        vmem = pl.BlockSpec(memory_space=pltpu.VMEM)
        dma = pltpu.SemaphoreType.DMA
        return pl.pallas_call(
            functools.partial(kernel, n),
            out_shape=jax.ShapeDtypeStruct((1,) + tokens.shape, bf16),
            in_specs=[vmem, vmem, any_, any_, any_, any_, any_, vmem, any_, any_, vmem],
            out_specs=vmem,
            scratch_shapes=[
                pltpu.VMEM((9, BLK, width), bf16),
                pltpu.VMEM((3 * BLK, width), bf16),
                pltpu.VMEM((BLK, width), bf16),
                pltpu.VMEM((9 * BLK, width), bf16),
                pltpu.VMEM((9 * BLK, width), bf16),
                pltpu.VMEM((BLK, width), bf16),
                pltpu.VMEM((BLK, width), bf16),
                pltpu.VMEM((GROUP, BLK, width), bf16),
                pltpu.VMEM((BLK, held), bf16),
                pltpu.VMEM((BLK, width), f32),
                pltpu.VMEM((GROUP, BLK, width), bf16),
                pltpu.VMEM((GROUP, BLK, width), bf16),
                pltpu.VMEM((BLK, width), bf16),
                pltpu.VMEM((width, width), bf16),
                pltpu.VMEM((width, width), bf16),
                pltpu.VMEM((width, width), bf16),
                pltpu.VMEM((width, width), bf16),
                pltpu.VMEM((held, width), bf16),
                pltpu.VMEM((held, width), bf16),
                dma((7,)),
                dma((9,)),
                dma((9,)),
                dma((9,)),
                dma((2 * members,)),
                dma((2 * members,)),
                dma((GROUP,)),
                dma((GROUP,)),
                dma((GROUP,)),
                dma((GROUP,)),
                pltpu.SemaphoreType.REGULAR,
            ],
            compiler_params=pltpu.CompilerParams(
                collective_id=0, has_side_effects=True, vmem_limit_bytes=48 * 1024 * 1024),
        )(ids, count.reshape(1, 1), tokens, w_query, w_key, w_value, w_out, gain, w_up, w_down, second_gain)

    in_specs = (
        P(None, "seq", None),
        P("seq", None),
        P("seq"),
        P("section", None, None),
        P("section", None, None),
        P("section", None, None),
        P("section", None, None),
        P("section", None),
        P("section", "seq", None),
        P("section", "seq", None),
        P("section", None),
    )
    return jax.shard_map(
        local, mesh=mesh, in_specs=in_specs, out_specs=P("section", None, "seq", None), check_vma=False)
```

```python
import functools
import math

import jax
import jax.numpy as jnp
from jax import lax
from jax.experimental import pallas as pl
from jax.experimental.pallas import tpu as pltpu
from jax.sharding import PartitionSpec as P

HEADS = 16
BLK = 128
ROW = 4
GROUP = 4
TILE = 256
MESH = pl.DeviceIdType.MESH
NT = (((1,), (1,)), ((), ()))


def normalise(widened, gain):
    mean = jnp.mean(widened * widened, axis=-1, keepdims=True)
    return (widened * lax.rsqrt(mean + 1e-05) * gain).astype(jnp.bfloat16)


def kernel(
    n, ids, count, tokens, w_query, w_key, w_value, w_out, gain, w_up, w_down, second_gain,
    out,
    around, normed, queries, keys, values, mixed, attended, second, hidden, total, leaving,
    landing, finished, wq, wk, wv, wo, up, down,
    local_sem, x_send, x_recv, o_send, w_send, w_recv, s_send, s_recv, p_send, p_recv, go, f_send,
):
    section, seq = lax.axis_index("section"), lax.axis_index("seq")
    row, col = lax.div(seq, ROW), lax.rem(seq, ROW)
    rows = n // ROW
    width = wq.shape[0]
    units = w_up.shape[1]
    mine = lax.rem(row, GROUP)
    members = n // GROUP
    member = lax.div(row, GROUP) * ROW + col
    pairs = HEADS // 2
    tiles = width // TILE

    def local(src, dst, index):
        return pltpu.make_async_copy(src, dst, local_sem.at[index])

    own_up = pl.ds(pl.multiple_of(member * units, units), units)
    locals_ = [
        local(w_query.at[0], wq, 0),
        local(w_key.at[0], wk, 1),
        local(w_value.at[0], wv, 2),
        local(w_out.at[0], wo, 3),
        local(w_up.at[0], up.at[own_up], 4),
        local(w_down.at[0], down.at[own_up], 5),
    ]
    own_tokens = local(tokens.at[0], around.at[4], 6)

    @pl.when(section == 0)
    def _():
        own_tokens.start()

    for copy in locals_:
        copy.start()

    barrier = pltpu.get_barrier_semaphore()

    def greet(step, carry):
        other = lax.rem(section * n + seq + 1 + step, 2 * n)
        pl.semaphore_signal(barrier, inc=1, device_id=(lax.div(other, n), lax.rem(other, n)), device_id_type=MESH)
        return carry

    lax.fori_loop(0, 2 * n - 1, greet, 0)
    pl.semaphore_wait(barrier, 2 * n - 1)

    def beside(slot):
        dr, dc = slot // 3 - 1, slot % 3 - 1
        exists = (row + dr >= 0) & (row + dr < rows) & (col + dc >= 0) & (col + dc < ROW)
        return exists, jnp.clip(row + dr, 0, rows - 1) * ROW + jnp.clip(col + dc, 0, ROW - 1)

    def token_copy(slot):
        device = beside(slot)[1]
        return pltpu.make_async_remote_copy(
            around.at[4], around.at[8 - slot], x_send.at[slot], x_recv.at[8 - slot],
            device_id=(section, device), device_id_type=MESH)

    def result_copy(slot):
        device = beside(slot)[1]
        return pltpu.make_async_remote_copy(
            finished, around.at[8 - slot], o_send.at[slot], x_recv.at[8 - slot],
            device_id=(1, device), device_id_type=MESH)

    def relay(index):
        side, up_or_down = index % 2 * 2, index // 2 * 2
        device = beside(3 * up_or_down + 1)[1]
        slot = 3 * (2 - up_or_down) + side
        exists = beside(3 + side)[0] & beside(3 * up_or_down + 1)[0]
        return exists, pltpu.make_async_remote_copy(
            around.at[3 + side], around.at[slot], f_send.at[index], x_recv.at[slot],
            device_id=(section, device), device_id_type=MESH)

    def arrival(slot):
        return pltpu.make_async_remote_copy(
            finished, around.at[slot], o_send.at[slot], x_recv.at[slot],
            device_id=(section, seq), device_id_type=MESH)

    def weight_copies(step, which):
        place = lax.rem(member + step, members)
        device = (lax.div(place, ROW) * GROUP + mine) * ROW + lax.rem(place, ROW)
        src, dst = (w_up, up) if which == 0 else (w_down, down)
        return pltpu.make_async_remote_copy(
            src.at[0], dst.at[own_up], w_send.at[2 * step + which], w_recv.at[2 * step + which],
            device_id=(section, device), device_id_type=MESH)

    def weight_arrival(step, which):
        place = lax.rem(member + members - step, members)
        there = pl.ds(pl.multiple_of(place * units, units), units)
        src, dst = (w_up, up) if which == 0 else (w_down, down)
        return pltpu.make_async_remote_copy(
            src.at[0], dst.at[there], w_send.at[2 * step + which], w_recv.at[2 * step + which],
            device_id=(section, seq), device_id_type=MESH)

    def each(body):
        if members > 8:
            lax.fori_loop(1, members, body, 0)
        else:
            for step in range(1, members):
                body(step, 0)

    @pl.when(section == 0)
    def _():
        own_tokens.wait()
        for slot in (3, 5, 1, 7):
            @pl.when(beside(slot)[0])
            def _():
                token_copy(slot).start()

    @pl.when(section == 1)
    def _():
        pl.semaphore_wait(go, 1)

    def send_weights(step, carry):
        weight_copies(step, 0).start()
        weight_copies(step, 1).start()
        return carry

    each(send_weights)

    def await_slot(slot):
        exists = beside(slot)[0]

        @pl.when(exists)
        def _():
            arrival(slot).wait_recv()

        @pl.when(jnp.logical_not(exists))
        def _():
            around[slot] = jnp.zeros((BLK, width), jnp.bfloat16)

    @pl.when(section == 1)
    def _():
        arrival(4).wait_recv()

    entries = ids[...]
    listed = lax.broadcasted_iota(jnp.int32, entries.shape, 1) < count[...]
    flags = []
    for slot in range(9):
        exists, device = beside(slot)
        wanted = jnp.where(exists, device, jnp.int32(-1))
        hit = jnp.where(listed & (entries == wanted), 1.0, 0.0)
        flags.append(jnp.broadcast_to(jnp.max(hit, axis=1, keepdims=True), (1, BLK)))
    live_row = jnp.concatenate(flags, axis=1)

    gain_row = gain[...]
    normed[pl.ds(0, BLK)] = normalise(around[4].astype(jnp.float32), gain_row)
    locals_[0].wait()

    score_scale = 1.0 / math.sqrt(width // HEADS)

    def query_tile(step, carry):
        at = pl.ds(pl.multiple_of(step * TILE, TILE), TILE)
        product = jnp.dot(normed[pl.ds(0, BLK)], wq[:, at], preferred_element_type=jnp.float32)
        queries[:, at] = (product.astype(jnp.bfloat16).astype(jnp.float32) * score_scale).astype(jnp.bfloat16)
        return carry

    lax.fori_loop(0, tiles, query_tile, 0)
    locals_[1].wait()
    locals_[2].wait()

    for part in (1, 0, 2):
        for slot in range(3 * part, 3 * part + 3):
            if slot != 4:
                await_slot(slot)
            for index in range(4):
                if slot == 3 + index % 2 * 2:
                    @pl.when(relay(index)[0])
                    def _():
                        relay(index)[1].start()
        for slot in range(3):
            normed[pl.ds(slot * BLK, BLK)] = normalise(
                around[3 * part + slot].astype(jnp.float32), gain_row)

        def key_tile(step, carry):
            at = pl.ds(pl.multiple_of(step * TILE, TILE), TILE)
            there = pl.ds(3 * part * BLK, 3 * BLK)
            keys[there, at] = jnp.dot(
                normed[...], wk[:, at], preferred_element_type=jnp.float32).astype(jnp.bfloat16)
            values[there, at] = jnp.dot(
                normed[...], wv[:, at], preferred_element_type=jnp.float32).astype(jnp.bfloat16)
            return carry

        lax.fori_loop(0, tiles, key_tile, 0)

    first_half = lax.broadcasted_iota(jnp.int32, (BLK, 128), 1) < 64

    def head_pair(pair, carry):
        at = pl.ds(pl.multiple_of(pair * 128, 128), 128)
        q = queries[:, at]
        zero = jnp.zeros_like(q)
        both = jnp.concatenate([jnp.where(first_half, q, zero), jnp.where(first_half, zero, q)], axis=0)
        scores = lax.dot_general(both, keys[:, at], NT, preferred_element_type=jnp.float32)
        scores = jnp.where(live_row > 0.0, scores, -jnp.inf)
        exponent = jnp.exp(scores - jnp.max(scores, axis=-1, keepdims=True))
        divisor = jnp.sum(exponent, axis=-1, keepdims=True)
        product = jnp.dot(
            exponent.astype(jnp.bfloat16), values[:, at], preferred_element_type=jnp.float32) / divisor
        mixed[:, at] = jnp.where(first_half, product[:BLK], product[BLK:]).astype(jnp.bfloat16)
        return carry

    lax.fori_loop(0, pairs, head_pair, 0)
    locals_[3].wait()

    def out_tile(step, carry):
        at = pl.ds(pl.multiple_of(step * TILE, TILE), TILE)
        product = jnp.dot(mixed[...], wo[:, at], preferred_element_type=jnp.float32)
        attended[:, at] = (around[4, :, at].astype(jnp.float32) + product).astype(jnp.bfloat16)
        return carry

    lax.fori_loop(0, tiles, out_tile, 0)
    second[mine] = normalise(attended[...].astype(jnp.float32), second_gain[...])

    def peer(step):
        return lax.rem(mine + step, GROUP)

    def peer_device(step):
        return (lax.div(row, GROUP) * GROUP + peer(step)) * ROW + col

    def second_copy(step):
        return pltpu.make_async_remote_copy(
            second.at[mine], second.at[mine], s_send.at[step], s_recv.at[step],
            device_id=(section, peer_device(step)), device_id_type=MESH)

    def second_arrival(step):
        return pltpu.make_async_remote_copy(
            second.at[mine], second.at[peer(step)], s_send.at[step], s_recv.at[GROUP - step],
            device_id=(section, peer_device(step)), device_id_type=MESH)

    def partial_copy(step):
        return pltpu.make_async_remote_copy(
            leaving.at[step], landing.at[step], p_send.at[step], p_recv.at[step],
            device_id=(section, peer_device(step)), device_id_type=MESH)

    for step in range(1, GROUP):
        second_copy(step).start()

    locals_[4].wait()
    locals_[5].wait()

    def await_weights(step, carry):
        weight_arrival(step, 0).wait_recv()
        weight_arrival(step, 1).wait_recv()
        return carry

    each(await_weights)

    @pl.when(section == 0)
    def _():
        pl.semaphore_signal(go, inc=1, device_id=(1, seq), device_id_type=MESH)

    for step in range(GROUP):
        if step:
            second_arrival(step).wait_recv()
        rows_in = second.at[peer(step)]

        def up_tile(tile, carry):
            at = pl.ds(pl.multiple_of(tile * TILE, TILE), TILE)
            raised = lax.dot_general(rows_in[...], up[at], NT, preferred_element_type=jnp.float32)
            hidden[:, at] = jax.nn.gelu(raised, approximate=True).astype(jnp.bfloat16)
            return carry

        lax.fori_loop(0, up.shape[0] // TILE, up_tile, 0)

        def down_tile(tile, carry):
            at = pl.ds(pl.multiple_of(tile * TILE, TILE), TILE)
            product = jnp.dot(hidden[...], down[:, at], preferred_element_type=jnp.float32)
            if step:
                leaving[step, :, at] = product.astype(jnp.bfloat16)
            else:
                total[:, at] = product
            return carry

        lax.fori_loop(0, tiles, down_tile, 0)
        if step:
            partial_copy(step).start()

    gathered = attended[...].astype(jnp.float32) + total[...]
    for step in range(1, GROUP):
        partial_copy(step).wait_recv()
        gathered = gathered + landing[step].astype(jnp.float32)
    result = gathered.astype(jnp.bfloat16)
    finished[...] = result
    out[0, 0] = result

    @pl.when(section == 0)
    def _():
        for slot in (4, 3, 5, 1, 7):
            @pl.when(beside(slot)[0])
            def _():
                result_copy(slot).start()
        for slot in (4, 3, 5, 1, 7):
            @pl.when(beside(slot)[0])
            def _():
                result_copy(slot).wait_send()
                if slot != 4:
                    token_copy(slot).wait_send()

    for index in range(4):
        @pl.when(relay(index)[0])
        def _():
            relay(index)[1].wait_send()

    for step in range(1, GROUP):
        second_copy(step).wait_send()
        partial_copy(step).wait_send()

    def drain(step, carry):
        weight_copies(step, 0).wait_send()
        weight_copies(step, 1).wait_send()
        return carry

    each(drain)


def solution(mesh):
    n = mesh.shape["seq"]

    def local(tokens, ids, count, w_query, w_key, w_value, w_out, gain, w_up, w_down, second_gain):
        width = tokens.shape[-1]
        held = w_up.shape[1] * n // GROUP
        members = n // GROUP
        bf16, f32 = jnp.bfloat16, jnp.float32
        any_ = pl.BlockSpec(memory_space=pltpu.HBM)
        vmem = pl.BlockSpec(memory_space=pltpu.VMEM)
        dma = pltpu.SemaphoreType.DMA
        return pl.pallas_call(
            functools.partial(kernel, n),
            out_shape=jax.ShapeDtypeStruct((1,) + tokens.shape, bf16),
            in_specs=[vmem, vmem, any_, any_, any_, any_, any_, vmem, any_, any_, vmem],
            out_specs=vmem,
            scratch_shapes=[
                pltpu.VMEM((9, BLK, width), bf16),
                pltpu.VMEM((3 * BLK, width), bf16),
                pltpu.VMEM((BLK, width), bf16),
                pltpu.VMEM((9 * BLK, width), bf16),
                pltpu.VMEM((9 * BLK, width), bf16),
                pltpu.VMEM((BLK, width), bf16),
                pltpu.VMEM((BLK, width), bf16),
                pltpu.VMEM((GROUP, BLK, width), bf16),
                pltpu.VMEM((BLK, held), bf16),
                pltpu.VMEM((BLK, width), f32),
                pltpu.VMEM((GROUP, BLK, width), bf16),
                pltpu.VMEM((GROUP, BLK, width), bf16),
                pltpu.VMEM((BLK, width), bf16),
                pltpu.VMEM((width, width), bf16),
                pltpu.VMEM((width, width), bf16),
                pltpu.VMEM((width, width), bf16),
                pltpu.VMEM((width, width), bf16),
                pltpu.VMEM((held, width), bf16),
                pltpu.VMEM((held, width), bf16),
                dma((7,)),
                dma((9,)),
                dma((9,)),
                dma((9,)),
                dma((2 * members,)),
                dma((2 * members,)),
                dma((GROUP,)),
                dma((GROUP,)),
                dma((GROUP,)),
                dma((GROUP,)),
                pltpu.SemaphoreType.REGULAR,
                dma((4,)),
            ],
            compiler_params=pltpu.CompilerParams(
                collective_id=0, has_side_effects=True, vmem_limit_bytes=56 * 1024 * 1024),
        )(ids, count.reshape(1, 1), tokens, w_query, w_key, w_value, w_out, gain, w_up, w_down, second_gain)

    in_specs = (
        P(None, "seq", None),
        P("seq", None),
        P("seq"),
        P("section", None, None),
        P("section", None, None),
        P("section", None, None),
        P("section", None, None),
        P("section", None),
        P("section", "seq", None),
        P("section", "seq", None),
        P("section", None),
    )
    return jax.shard_map(
        local, mesh=mesh, in_specs=in_specs, out_specs=P("section", None, "seq", None), check_vma=False)
```

```python
import functools
import math

import jax
import jax.numpy as jnp
from jax import lax
from jax.experimental import pallas as pl
from jax.experimental.pallas import tpu as pltpu
from jax.sharding import PartitionSpec as P

HEADS = 16
BLK = 128
ROW = 4
GROUP = 4
TILE = 256
MESH = pl.DeviceIdType.MESH
NT = (((1,), (1,)), ((), ()))


def normalise(widened, gain):
    mean = jnp.mean(widened * widened, axis=-1, keepdims=True)
    return (widened * lax.rsqrt(mean + 1e-05) * gain).astype(jnp.bfloat16)


def kernel(
    n, ids, count, tokens, w_query, w_key, w_value, w_out, gain, w_up, w_down, second_gain,
    out,
    around, normed, queries, keys, values, mixed, attended, second, hidden, total, leaving,
    landing, finished, wq, wk, wv, wo, up, down,
    local_sem, x_send, x_recv, o_send, w_send, w_recv, s_send, s_recv, p_send, p_recv, go, f_send,
):
    section, seq = lax.axis_index("section"), lax.axis_index("seq")
    row, col = lax.div(seq, ROW), lax.rem(seq, ROW)
    rows = n // ROW
    width = wq.shape[0]
    units = w_up.shape[1]
    mine = lax.rem(row, GROUP)
    members = n // GROUP
    member = lax.div(row, GROUP) * ROW + col
    pairs = HEADS // 2
    tiles = width // TILE

    def local(src, dst, index):
        return pltpu.make_async_copy(src, dst, local_sem.at[index])

    own_up = pl.ds(pl.multiple_of(member * units, units), units)
    locals_ = [
        local(w_query.at[0], wq, 0),
        local(w_key.at[0], wk, 1),
        local(w_value.at[0], wv, 2),
        local(w_out.at[0], wo, 3),
        local(w_up.at[0], up.at[own_up], 4),
        local(w_down.at[0], down.at[own_up], 5),
    ]
    own_tokens = local(tokens.at[0], around.at[4], 6)

    @pl.when(section == 0)
    def _():
        own_tokens.start()

    for copy in locals_:
        copy.start()

    barrier = pltpu.get_barrier_semaphore()

    def greet(step, carry):
        other = lax.rem(section * n + seq + 1 + step, 2 * n)
        pl.semaphore_signal(barrier, inc=1, device_id=(lax.div(other, n), lax.rem(other, n)), device_id_type=MESH)
        return carry

    lax.fori_loop(0, 2 * n - 1, greet, 0)
    pl.semaphore_wait(barrier, 2 * n - 1)

    def beside(slot):
        dr, dc = slot // 3 - 1, slot % 3 - 1
        exists = (row + dr >= 0) & (row + dr < rows) & (col + dc >= 0) & (col + dc < ROW)
        return exists, jnp.clip(row + dr, 0, rows - 1) * ROW + jnp.clip(col + dc, 0, ROW - 1)

    def token_copy(slot):
        device = beside(slot)[1]
        return pltpu.make_async_remote_copy(
            around.at[4], around.at[8 - slot], x_send.at[slot], x_recv.at[8 - slot],
            device_id=(section, device), device_id_type=MESH)

    def result_copy(slot):
        device = beside(slot)[1]
        return pltpu.make_async_remote_copy(
            finished, around.at[8 - slot], o_send.at[slot], x_recv.at[8 - slot],
            device_id=(1, device), device_id_type=MESH)

    def relay(index):
        side, up_or_down = index % 2 * 2, index // 2 * 2
        device = beside(3 * up_or_down + 1)[1]
        slot = 3 * (2 - up_or_down) + side
        exists = beside(3 + side)[0] & beside(3 * up_or_down + 1)[0]
        return exists, pltpu.make_async_remote_copy(
            around.at[3 + side], around.at[slot], f_send.at[index], x_recv.at[slot],
            device_id=(section, device), device_id_type=MESH)

    def arrival(slot):
        return pltpu.make_async_remote_copy(
            finished, around.at[slot], o_send.at[slot], x_recv.at[slot],
            device_id=(section, seq), device_id_type=MESH)

    def weight_copies(step, which):
        place = lax.rem(member + step, members)
        device = (lax.div(place, ROW) * GROUP + mine) * ROW + lax.rem(place, ROW)
        src, dst = (w_up, up) if which == 0 else (w_down, down)
        return pltpu.make_async_remote_copy(
            src.at[0], dst.at[own_up], w_send.at[2 * step + which], w_recv.at[2 * step + which],
            device_id=(section, device), device_id_type=MESH)

    def weight_arrival(step, which):
        place = lax.rem(member + members - step, members)
        there = pl.ds(pl.multiple_of(place * units, units), units)
        src, dst = (w_up, up) if which == 0 else (w_down, down)
        return pltpu.make_async_remote_copy(
            src.at[0], dst.at[there], w_send.at[2 * step + which], w_recv.at[2 * step + which],
            device_id=(section, seq), device_id_type=MESH)

    def each(body):
        if members > 8:
            lax.fori_loop(1, members, body, 0)
        else:
            for step in range(1, members):
                body(step, 0)

    @pl.when(section == 0)
    def _():
        own_tokens.wait()
        for slot in (3, 5, 1, 7):
            @pl.when(beside(slot)[0])
            def _():
                token_copy(slot).start()

    @pl.when(section == 1)
    def _():
        pl.semaphore_wait(go, 1)

    def send_weights(step, carry):
        weight_copies(step, 0).start()
        weight_copies(step, 1).start()
        return carry

    each(send_weights)

    def await_slot(slot):
        exists = beside(slot)[0]

        @pl.when(exists)
        def _():
            arrival(slot).wait_recv()

        @pl.when(jnp.logical_not(exists))
        def _():
            around[slot] = jnp.zeros((BLK, width), jnp.bfloat16)

    @pl.when(section == 1)
    def _():
        arrival(4).wait_recv()

    entries = ids[...]
    listed = lax.broadcasted_iota(jnp.int32, entries.shape, 1) < count[...]
    flags = []
    for slot in range(9):
        exists, device = beside(slot)
        wanted = jnp.where(exists, device, jnp.int32(-1))
        hit = jnp.where(listed & (entries == wanted), 1.0, 0.0)
        flags.append(jnp.broadcast_to(jnp.max(hit, axis=1, keepdims=True), (1, BLK)))
    live_row = jnp.concatenate(flags, axis=1)

    gain_row = gain[...]
    normed[pl.ds(0, BLK)] = normalise(around[4].astype(jnp.float32), gain_row)
    locals_[0].wait()

    score_scale = 1.0 / math.sqrt(width // HEADS)

    def query_tile(step, carry):
        at = pl.ds(pl.multiple_of(step * TILE, TILE), TILE)
        product = jnp.dot(normed[pl.ds(0, BLK)], wq[:, at], preferred_element_type=jnp.float32)
        queries[:, at] = (product.astype(jnp.bfloat16).astype(jnp.float32) * score_scale).astype(jnp.bfloat16)
        return carry

    lax.fori_loop(0, tiles, query_tile, 0)
    locals_[1].wait()
    locals_[2].wait()

    for part in (1, 0, 2):
        for slot in range(3 * part, 3 * part + 3):
            if slot != 4:
                await_slot(slot)
            for index in range(4):
                if slot == 3 + index % 2 * 2:
                    @pl.when(relay(index)[0])
                    def _():
                        relay(index)[1].start()
        for slot in range(3):
            normed[pl.ds(slot * BLK, BLK)] = normalise(
                around[3 * part + slot].astype(jnp.float32), gain_row)

        def key_tile(step, carry):
            at = pl.ds(pl.multiple_of(step * TILE, TILE), TILE)
            there = pl.ds(3 * part * BLK, 3 * BLK)
            keys[there, at] = jnp.dot(
                normed[...], wk[:, at], preferred_element_type=jnp.float32).astype(jnp.bfloat16)
            values[there, at] = jnp.dot(
                normed[...], wv[:, at], preferred_element_type=jnp.float32).astype(jnp.bfloat16)
            return carry

        lax.fori_loop(0, tiles, key_tile, 0)

    first_half = lax.broadcasted_iota(jnp.int32, (BLK, 128), 1) < 64

    def head_pair(pair, carry):
        at = pl.ds(pl.multiple_of(pair * 128, 128), 128)
        q = queries[:, at]
        zero = jnp.zeros_like(q)
        both = jnp.concatenate([jnp.where(first_half, q, zero), jnp.where(first_half, zero, q)], axis=0)
        scores = lax.dot_general(both, keys[:, at], NT, preferred_element_type=jnp.float32)
        scores = jnp.where(live_row > 0.0, scores, -jnp.inf)
        exponent = jnp.exp(scores - jnp.max(scores, axis=-1, keepdims=True))
        divisor = jnp.sum(exponent, axis=-1, keepdims=True)
        product = jnp.dot(
            exponent.astype(jnp.bfloat16), values[:, at], preferred_element_type=jnp.float32) / divisor
        mixed[:, at] = jnp.where(first_half, product[:BLK], product[BLK:]).astype(jnp.bfloat16)
        return carry

    lax.fori_loop(0, pairs, head_pair, 0)
    locals_[3].wait()

    def out_tile(step, carry):
        at = pl.ds(pl.multiple_of(step * TILE, TILE), TILE)
        product = jnp.dot(mixed[...], wo[:, at], preferred_element_type=jnp.float32)
        attended[:, at] = (around[4, :, at].astype(jnp.float32) + product).astype(jnp.bfloat16)
        return carry

    lax.fori_loop(0, tiles, out_tile, 0)
    second[mine] = normalise(attended[...].astype(jnp.float32), second_gain[...])

    def peer(step):
        if step == 1:
            return mine + 1 - 2 * lax.rem(mine, 2)
        return mine if step == 0 else lax.rem(mine + 2, GROUP) if step == 2 else GROUP - 1 - mine

    def peer_device(step):
        return (lax.div(row, GROUP) * GROUP + peer(step)) * ROW + col

    def second_copy(step):
        return pltpu.make_async_remote_copy(
            second.at[mine], second.at[mine], s_send.at[step], s_recv.at[step],
            device_id=(section, peer_device(step)), device_id_type=MESH)

    def second_arrival(step):
        return pltpu.make_async_remote_copy(
            second.at[mine], second.at[peer(step)], s_send.at[step], s_recv.at[step],
            device_id=(section, peer_device(step)), device_id_type=MESH)

    def partial_copy(step):
        return pltpu.make_async_remote_copy(
            leaving.at[step], landing.at[step], p_send.at[step], p_recv.at[step],
            device_id=(section, peer_device(step)), device_id_type=MESH)

    for step in range(1, GROUP):
        second_copy(step).start()

    locals_[4].wait()
    locals_[5].wait()

    def await_weights(step, carry):
        weight_arrival(step, 0).wait_recv()
        weight_arrival(step, 1).wait_recv()
        return carry

    each(await_weights)

    @pl.when(section == 0)
    def _():
        pl.semaphore_signal(go, inc=1, device_id=(1, seq), device_id_type=MESH)

    for step in range(GROUP):
        if step:
            second_arrival(step).wait_recv()
        rows_in = second.at[peer(step)]

        def up_tile(tile, carry):
            at = pl.ds(pl.multiple_of(tile * TILE, TILE), TILE)
            raised = lax.dot_general(rows_in[...], up[at], NT, preferred_element_type=jnp.float32)
            hidden[:, at] = jax.nn.gelu(raised, approximate=True).astype(jnp.bfloat16)
            return carry

        lax.fori_loop(0, up.shape[0] // TILE, up_tile, 0)

        def down_tile(tile, carry):
            at = pl.ds(pl.multiple_of(tile * TILE, TILE), TILE)
            product = jnp.dot(hidden[...], down[:, at], preferred_element_type=jnp.float32)
            if step:
                leaving[step, :, at] = product.astype(jnp.bfloat16)
            else:
                total[:, at] = product
            return carry

        lax.fori_loop(0, tiles, down_tile, 0)
        if step:
            partial_copy(step).start()

    gathered = attended[...].astype(jnp.float32) + total[...]
    for step in range(1, GROUP):
        partial_copy(step).wait_recv()
        gathered = gathered + landing[step].astype(jnp.float32)
    result = gathered.astype(jnp.bfloat16)
    finished[...] = result
    out[0, 0] = result

    @pl.when(section == 0)
    def _():
        for slot in (4, 3, 5, 1, 7):
            @pl.when(beside(slot)[0])
            def _():
                result_copy(slot).start()
        for slot in (4, 3, 5, 1, 7):
            @pl.when(beside(slot)[0])
            def _():
                result_copy(slot).wait_send()
                if slot != 4:
                    token_copy(slot).wait_send()

    for index in range(4):
        @pl.when(relay(index)[0])
        def _():
            relay(index)[1].wait_send()

    for step in range(1, GROUP):
        second_copy(step).wait_send()
        partial_copy(step).wait_send()

    def drain(step, carry):
        weight_copies(step, 0).wait_send()
        weight_copies(step, 1).wait_send()
        return carry

    each(drain)


def solution(mesh):
    n = mesh.shape["seq"]

    def local(tokens, ids, count, w_query, w_key, w_value, w_out, gain, w_up, w_down, second_gain):
        width = tokens.shape[-1]
        held = w_up.shape[1] * n // GROUP
        members = n // GROUP
        bf16, f32 = jnp.bfloat16, jnp.float32
        any_ = pl.BlockSpec(memory_space=pltpu.HBM)
        vmem = pl.BlockSpec(memory_space=pltpu.VMEM)
        dma = pltpu.SemaphoreType.DMA
        return pl.pallas_call(
            functools.partial(kernel, n),
            out_shape=jax.ShapeDtypeStruct((1,) + tokens.shape, bf16),
            in_specs=[vmem, vmem, any_, any_, any_, any_, any_, vmem, any_, any_, vmem],
            out_specs=vmem,
            scratch_shapes=[
                pltpu.VMEM((9, BLK, width), bf16),
                pltpu.VMEM((3 * BLK, width), bf16),
                pltpu.VMEM((BLK, width), bf16),
                pltpu.VMEM((9 * BLK, width), bf16),
                pltpu.VMEM((9 * BLK, width), bf16),
                pltpu.VMEM((BLK, width), bf16),
                pltpu.VMEM((BLK, width), bf16),
                pltpu.VMEM((GROUP, BLK, width), bf16),
                pltpu.VMEM((BLK, held), bf16),
                pltpu.VMEM((BLK, width), f32),
                pltpu.VMEM((GROUP, BLK, width), bf16),
                pltpu.VMEM((GROUP, BLK, width), bf16),
                pltpu.VMEM((BLK, width), bf16),
                pltpu.VMEM((width, width), bf16),
                pltpu.VMEM((width, width), bf16),
                pltpu.VMEM((width, width), bf16),
                pltpu.VMEM((width, width), bf16),
                pltpu.VMEM((held, width), bf16),
                pltpu.VMEM((held, width), bf16),
                dma((7,)),
                dma((9,)),
                dma((9,)),
                dma((9,)),
                dma((2 * members,)),
                dma((2 * members,)),
                dma((GROUP,)),
                dma((GROUP,)),
                dma((GROUP,)),
                dma((GROUP,)),
                pltpu.SemaphoreType.REGULAR,
                dma((4,)),
            ],
            compiler_params=pltpu.CompilerParams(
                collective_id=0, has_side_effects=True, vmem_limit_bytes=56 * 1024 * 1024),
        )(ids, count.reshape(1, 1), tokens, w_query, w_key, w_value, w_out, gain, w_up, w_down, second_gain)

    in_specs = (
        P(None, "seq", None),
        P("seq", None),
        P("seq"),
        P("section", None, None),
        P("section", None, None),
        P("section", None, None),
        P("section", None, None),
        P("section", None),
        P("section", "seq", None),
        P("section", "seq", None),
        P("section", None),
    )
    return jax.shard_map(
        local, mesh=mesh, in_specs=in_specs, out_specs=P("section", None, "seq", None), check_vma=False)
```
